32 devices in a mesh: groups: 2 (over y), rank: 16 (over z, x, core).
Axes of the slice: x: 2, y: 2, z: 4, core: 2. Of those that a mesh axis runs over, the one named last changes fastest.
Arguments:
- pool: bfloat16 [512, 1024], P(('groups', 'rank')), parts along dimension 0, may hold values from -6 to 6
- kv_cache: bfloat16 [128, 4, 64, 256], P(('groups', 'rank')), parts along dimension 0
- w_qu: bfloat16 [1024, 1024], replicated, may hold values from -0.1875 to 0.1875
- w_out: bfloat16 [512, 1024], replicated, may hold values from -0.25 to 0.25
- norm_gain: float32 [512], replicated, may hold values from 0.1 to 1.9
- cand_ids: int32 [8, 2048], P('groups'), parts along dimension 0, may hold values from 0 to 255
- ranker: int32 [4], replicated, may hold values from 0 to 3, each once
- hist_blocks: int32 [8], P('groups'), parts along dimension 0, may hold values from 4 to 16, as said below
- cache_slot: int32 [8, 16], P('groups'), parts along dimension 0, may hold values from 0 to 63, as said below
Outputs:
- ranked: bfloat16 [16384, 1024], P(('groups', 'rank')), parts along dimension 0
The draws below stay inside these ranges and needn't reach their ends.
There are 2 independent parts, one for each index of `groups`. The reference program is written for one: setup_inputs(seed, part) draws one part's arguments, and reference() takes and returns one part's arrays. A program takes and returns all parts, laid end to end along the dimension named above; an argument that names none is the same for every part. Nothing has to cross between parts.
Inputs may be any that keep to these rules, and one draw needn't show every extreme that they name: Block b of user u (b < 16) is held in slot cache_slot[u, b], which lies on device cache_slot[u, b] // 4 of the rank axis. Each slot holds exactly one pair (u, b); the 16 blocks of one user lie on 16 different devices. `ranker`: each ranking group scores exactly one user. User u's history is its blocks 0 to hist_blocks[u] - 1; its other blocks are unused. Some user has 16 blocks.
All inputs are finite; a program needn't handle non-finite values.
Results may differ from the reference program's by a relative error of at most 0.0054.
Values may be sent and summed in bfloat16 or wider, within the bound.
No kernel may reach another device: no remote copies, remote signals or barrier semaphores. Data moves between devices by JAX's collectives and lax.ppermute only.
A program may use at most 128 MiB of HBM per device.

```python
import jax
import jax.numpy as jnp
from jax import lax

D = 1024
HEADS = 4
HEAD_DIM = 128
BLOCK = 64
CAND = 2048
HB = 16
USERS = 4
BLK_DEV = 4
SLOTS = 64
POOL = 256
N_RANK = 16


def draw_cache_slot(key, part):
    key_order, key_turn, key_owner = jax.random.split(jax.random.fold_in(key, 11), 3)
    user_order = jax.random.permutation(key_order, USERS)
    user_class = user_order // BLK_DEV
    slot_place = user_order % BLK_DEV
    rotation = jax.random.randint(key_turn, (USERS,), 0, HB)
    owner_order = jax.random.permutation(key_owner, N_RANK)
    position = user_class[:, None] * HB + (jnp.arange(HB)[None, :] + rotation[:, None]) % HB
    owners = owner_order[position]
    return (owners * BLK_DEV + slot_place[:, None]).astype(jnp.int32)


def draw_hist_blocks(key, part):
    key_length, key_pick = jax.random.split(jax.random.fold_in(key, 23))
    lengths = jax.random.randint(key_length, (USERS,), HB // 4, HB + 1)
    chosen = jax.random.permutation(key_pick, USERS)
    lengths = lengths.at[chosen[0]].set(HB).at[chosen[1]].set(HB // 4)
    return lengths.astype(jnp.int32)


def draw_kv_cache(key, part):
    key_base, key_column = jax.random.split(jax.random.fold_in(key, 37))
    array_shape = (SLOTS, HEADS, BLOCK, 2 * HEAD_DIM)
    column_draw = jax.random.uniform(key_column, (HEADS, 2 * HEAD_DIM), jnp.float32)
    head_place = jnp.arange(HEADS, dtype=jnp.float32) / (HEADS - 1)
    is_value = jnp.arange(2 * HEAD_DIM) >= HEAD_DIM
    base_draw = jax.random.normal(key_base, array_shape, jnp.float32)
    key_scale = 0.5 * 4.0 ** column_draw
    value_scale = 10.0 ** column_draw * (2.0 ** head_place)[:, None]
    factor = jnp.where(is_value[None, :], value_scale, key_scale)
    return (base_draw * factor[None, :, None, :]).astype(jnp.bfloat16)


def with_ends(array, stream_key, low, largest):
    index_at = [jax.random.randint(jax.random.fold_in(stream_key, axis), (), 0, length) for axis, length in enumerate(array.shape)]
    main_axis = array.shape.index(max(array.shape))
    next_to = index_at[:main_axis] + [(index_at[main_axis] + 1) % array.shape[main_axis]] + index_at[main_axis + 1:]
    return array.at[tuple(index_at)].set(low).at[tuple(next_to)].set(largest)


def level_of(own_key, dims, cuts, least, high):
    gain = 1.0
    for axis_at, shards_of in cuts:
        steps = jax.random.uniform(jax.random.fold_in(jax.random.fold_in(own_key, 6), axis_at), (shards_of,), jnp.float32, least / len(cuts), high / len(cuts))
        gain = gain * jnp.repeat(jnp.exp(steps), dims[axis_at] // shards_of).reshape((-1,) + (1,) * (len(dims) - 1 - axis_at))
    return gain


def normal_values(stream_key, shape, spread, most, cuts=(), kind=jnp.bfloat16):
    loudness = level_of(stream_key, shape, cuts, -0.22, 0.18) if cuts else 1.0
    array = jax.random.normal(stream_key, shape, jnp.float32) * spread * loudness
    return jnp.minimum(jnp.maximum(array, -most), most).astype(kind)


def setup_inputs(seed: int = 0, part: int = 0) -> dict:
    key_of = jax.random.split(jax.random.key(seed), 10)
    part_keys = jax.random.split(jax.random.fold_in(key_of[9], part), 10)
    return {
        "pool": normal_values(part_keys[0], (POOL, D), 1.0, 6.0, ((0, 16),)),
        "kv_cache": draw_kv_cache(jax.random.fold_in(jax.random.fold_in(key_of[9], part), 71), part),
        "w_qu": normal_values(key_of[2], (D, HEADS * 2 * HEAD_DIM), D ** -0.5, 0.1875),
        "w_out": normal_values(key_of[3], (HEADS * HEAD_DIM, D), (HEADS * HEAD_DIM) ** -0.5, 0.25),
        "norm_gain": jnp.clip(1.0 + 0.18 * jax.random.normal(key_of[4], (HEADS * HEAD_DIM,), jnp.float32), 0.1, 1.9),
        "cand_ids": with_ends(jax.random.randint(part_keys[5], (USERS, CAND), 0, POOL), jax.random.fold_in(part_keys[5], 1), 0, POOL - 1).astype(jnp.int32),
        "ranker": jax.random.permutation(key_of[6], USERS).astype(jnp.int32),
        "hist_blocks": draw_hist_blocks(jax.random.fold_in(jax.random.fold_in(key_of[9], part), 71), part),
        "cache_slot": draw_cache_slot(jax.random.fold_in(jax.random.fold_in(key_of[9], part), 71), part),
    }


norm_eps = 1e-05

def reference(pool, kv_cache, w_qu, w_out, norm_gain, cand_ids, ranker, hist_blocks, cache_slot):
    user_count = ranker.shape[0]
    user_range = jnp.arange(user_count, dtype=jnp.int32)
    user_of_group = jnp.zeros((user_count,), jnp.int32).at[ranker].set(user_range)
    score_scale = 1.0 / HEAD_DIM ** 0.5

    def one_user(user_index):
        cand_rows = jnp.take(pool, cand_ids[user_index], axis=0)
        head_qu = jax.nn.silu(jnp.dot(cand_rows, w_qu, preferred_element_type=jnp.float32)).astype(jnp.bfloat16)
        head_qu = head_qu.reshape(CAND, HEADS, 2, HEAD_DIM).astype(jnp.float32)
        queries = head_qu[:, :, 0, :]
        gates = head_qu[:, :, 1, :].reshape(CAND, HEADS * HEAD_DIM)
        history = jnp.take(kv_cache, cache_slot[user_index], axis=0)
        live_blocks = jnp.arange(HB) < hist_blocks[user_index]
        history = jnp.where(live_blocks[:, None, None, None], history, jnp.zeros_like(history))
        history = jnp.transpose(history, (1, 0, 2, 3)).reshape(HEADS, HB * BLOCK, 2 * HEAD_DIM).astype(jnp.float32)
        scores = jnp.einsum('chd,hkd->hck', queries, history[:, :, :HEAD_DIM])
        weights = jax.nn.silu(scores * score_scale).astype(jnp.bfloat16)
        weights = lax.optimization_barrier(weights).astype(jnp.float32)
        attended = jnp.einsum('hck,hkd->chd', weights, history[:, :, HEAD_DIM:]).reshape(CAND, HEADS * HEAD_DIM)
        mean_value = lax.optimization_barrier(jnp.mean(attended, axis=1, keepdims=True))
        variance = lax.optimization_barrier(jnp.mean(attended * attended, axis=1, keepdims=True)) - mean_value * mean_value
        hidden = ((attended - mean_value) * lax.rsqrt(variance + norm_eps) * norm_gain[None, :] * gates).astype(jnp.bfloat16)
        mixed = cand_rows.astype(jnp.float32) + jnp.dot(hidden, w_out, preferred_element_type=jnp.float32)
        return mixed.astype(jnp.bfloat16)
    results = lax.map(one_user, user_of_group)
    return results.reshape(USERS * CAND, D)
```

```python
import functools
import math

import jax
import jax.numpy as jnp
from jax import lax
from jax.experimental import pallas as pl
from jax.experimental.pallas import tpu as pltpu
from jax.sharding import PartitionSpec as P

norm_eps = 1e-05
VMEM = pl.BlockSpec(memory_space=pltpu.VMEM)
SMEM = pl.BlockSpec(memory_space=pltpu.SMEM)
ANY = pl.BlockSpec(memory_space=pl.ANY)


def swap_with(shard, mask):
    return lax.ppermute(shard, "rank", [(i, i ^ mask) for i in range(lax.axis_size("rank"))])


def call(kernel, out_shape, in_specs, scratch=(), flops=0, bytes_accessed=0, name=None):
    single = not isinstance(out_shape, (list, tuple))
    return pl.pallas_call(
        kernel,
        out_shape=out_shape,
        in_specs=in_specs,
        out_specs=VMEM if single else [VMEM] * len(out_shape),
        scratch_shapes=list(scratch),
        compiler_params=pltpu.CompilerParams(vmem_limit_bytes=48 * 1024 * 1024),
        cost_estimate=pl.CostEstimate(flops=flops, bytes_accessed=bytes_accessed, transcendentals=0),
        name=name,
    )


def pick_kernel(groups, group_size, me_ref, ranker_ref, slot_ref, kv_ref, *refs):
    outs, sem = refs[:-1], refs[-1]
    slots_here = kv_ref.shape[0]
    users, blocks = slot_ref.shape
    me = me_ref[0]
    my_group = me // group_size

    def slot_of(user):
        def step(b, found):
            local = slot_ref[user, b] - me * slots_here
            return jnp.where((local >= 0) & (local < slots_here), local, found)

        return lax.fori_loop(0, blocks, step, 0, unroll=blocks <= 16)

    def user_of(group):
        def step(u, found):
            return jnp.where(ranker_ref[u] == group, u, found)

        return lax.fori_loop(0, users, step, 0, unroll=users <= 16)

    copies = []
    for k in range(groups):
        slot = slot_of(user_of(my_group ^ k))
        copies.append(pltpu.make_async_copy(kv_ref.at[slot], outs[k], sem.at[k]))
        copies[-1].start()
    for copy in copies:
        copy.wait()


def project_kernel(heads, own_ref, far_ref, w_ref, q_ref, gate_ref):
    half = own_ref.shape[0]
    dim = w_ref.shape[1] // (2 * heads)
    for at, rows in ((0, own_ref), (half, far_ref)):
        qu = jax.nn.silu(jnp.dot(rows[...], w_ref[...], preferred_element_type=jnp.float32))
        qu = qu.astype(jnp.bfloat16)
        for h in range(heads):
            cols = slice(h * dim, (h + 1) * dim)
            q_ref[at : at + half, cols] = qu[:, 2 * h * dim : (2 * h + 1) * dim]
            gate_ref[at : at + half, cols] = qu[:, (2 * h + 1) * dim : (2 * h + 2) * dim]


def attend_kernel(groups, scale, live_ref, q_own_ref, q_far_ref, *refs):
    kv, own_ref, far_ref = refs[:groups], refs[groups], refs[groups + 1]
    heads, block, pair = kv[0].shape
    dim = pair // 2
    rows = q_own_ref.shape[0]
    tile = math.gcd(rows, 256)
    together = math.gcd(groups, 4)
    for q_ref, out_ref in ((q_far_ref, far_ref), (q_own_ref, own_ref)):

        def one_tile(t, _, q_ref=q_ref, out_ref=out_ref):
            at = pl.ds(pl.multiple_of(t * tile, tile), tile)
            for h in range(heads):
                cols = slice(h * dim, (h + 1) * dim)
                query = q_ref[at, cols]
                total = None
                for first in range(0, groups, together):
                    parts = []
                    for k in range(first, first + together):
                        part = kv[k][h]
                        parts.append(jnp.where(live_ref[k] > 0, part, jnp.zeros_like(part)))
                    keys = jnp.concatenate([p[:, :dim] for p in parts], axis=0)
                    values = jnp.concatenate([p[:, dim:] for p in parts], axis=0)
                    scores = lax.dot_general(
                        query, keys, (((1,), (1,)), ((), ())), preferred_element_type=jnp.float32
                    )
                    weights = jax.nn.silu(scores * scale).astype(jnp.bfloat16)
                    add = jnp.dot(weights, values, preferred_element_type=jnp.float32)
                    total = add if total is None else total + add
                out_ref[at, cols] = total
            return 0

        lax.fori_loop(0, rows // tile, one_tile, 0, unroll=rows == tile)


def finish_kernel(sum_ref, far_ref, gate_ref, own_ref, other_ref, gain_ref, w_ref, out_ref):
    half = own_ref.shape[0]
    tile = math.gcd(half, 64)
    for side, rows in ((0, own_ref), (1, other_ref)):
        for first in range(0, half, tile):
            mine = slice(side * half + first, side * half + first + tile)
            theirs = slice((1 - side) * half + first, (1 - side) * half + first + tile)
            attended = sum_ref[mine, :] + far_ref[theirs, :].astype(jnp.float32)
            mean = jnp.mean(attended, axis=1, keepdims=True)
            variance = jnp.mean(attended * attended, axis=1, keepdims=True) - mean * mean
            hidden = (attended - mean) * lax.rsqrt(variance + norm_eps) * gain_ref[...]
            hidden = (hidden * gate_ref[mine, :].astype(jnp.float32)).astype(jnp.bfloat16)
            mixed = jnp.dot(hidden, w_ref[...], preferred_element_type=jnp.float32)
            mixed = mixed + rows[first : first + tile, :].astype(jnp.float32)
            out_ref[mine, :] = mixed.astype(jnp.bfloat16)


def select_kernel(place_ref, own_ref, far_ref, out_ref):
    rows = own_ref.shape[0]
    place = place_ref[...]
    ids = lax.broadcasted_iota(jnp.int32, (place.shape[0], rows), 1)
    mine = (place == ids).astype(jnp.bfloat16)
    theirs = (place == ids + rows).astype(jnp.bfloat16)
    picked = jnp.dot(mine, own_ref[...], preferred_element_type=jnp.float32)
    picked = picked + jnp.dot(theirs, far_ref[...], preferred_element_type=jnp.float32)
    out_ref[...] = picked.astype(jnp.bfloat16)


def body(pool, kv_cache, w_qu, w_out, norm_gain, cand_ids, ranker, hist_blocks, cache_slot):
    devices = lax.axis_size("rank")
    me = lax.axis_index("rank")
    slots_here, heads, block, pair = kv_cache.shape
    dim = pair // 2
    users, blocks = cache_slot.shape
    pool_here, width = pool.shape
    groups = users
    size = devices // groups
    assert size == 4 and groups & (groups - 1) == 0
    my_group, my_place = me // size, me % size
    shape = jax.ShapeDtypeStruct

    block_shape = shape((heads, block, pair), jnp.bfloat16)
    picked = call(
        functools.partial(pick_kernel, groups, size),
        [block_shape] * groups,
        [SMEM, SMEM, SMEM, ANY],
        [pltpu.SemaphoreType.DMA((groups,))],
        bytes_accessed=2 * kv_cache.size * 2,
        name="pick",
    )(me.astype(jnp.int32).reshape(1), ranker, cache_slot, kv_cache)
    column = [pool] + [swap_with(pool, size * k) for k in range(1, groups)]
    kv = [picked[0]] + [swap_with(picked[k], size * k) for k in range(1, groups)]

    own_rows = jnp.concatenate(column, axis=0)
    far_rows = swap_with(own_rows, 2)
    rows = 2 * own_rows.shape[0]
    q_own, gates = call(
        functools.partial(project_kernel, heads),
        [shape((rows, heads * dim), jnp.bfloat16)] * 2,
        [VMEM] * 3,
        flops=2 * rows * width * w_qu.shape[1],
        bytes_accessed=w_qu.size * 2,
        name="project",
    )(own_rows, far_rows, w_qu)
    q_far = swap_with(q_own, 1)

    user_range = jnp.arange(users, dtype=jnp.int32)
    is_mine = ranker == my_group
    my_blocks = jnp.sum(jnp.where(is_mine, hist_blocks, 0))
    my_slots = jnp.sum(jnp.where(is_mine[:, None], cache_slot, 0), axis=0)
    source = (my_group ^ jnp.arange(groups, dtype=jnp.int32)) * size + my_place
    live = (my_slots[None, :] // slots_here == source[:, None]) & (
        jnp.arange(blocks, dtype=jnp.int32)[None, :] < my_blocks
    )
    live = jnp.any(live, axis=1).astype(jnp.int32)
    sums = shape((rows, heads * dim), jnp.float32)
    att_own, att_far = call(
        functools.partial(attend_kernel, groups, 1.0 / math.sqrt(dim)),
        [sums, sums],
        [SMEM] + [VMEM] * (2 + groups),
        flops=4 * 2 * rows * groups * block * heads * dim,
        bytes_accessed=groups * heads * block * pair * 2 + 4 * rows * heads * dim * 4,
        name="attend",
    )(live, q_own, q_far, *kv)

    att_own = att_own + swap_with(att_far, 1)
    att_sent = swap_with(att_own.astype(jnp.bfloat16), 2)
    table = call(
        finish_kernel,
        shape((rows, width), jnp.bfloat16),
        [VMEM] * 7,
        flops=2 * rows * heads * dim * width,
        bytes_accessed=w_out.size * 2,
        name="finish",
    )(att_own, att_sent, gates, own_rows, far_rows, norm_gain[None, :], w_out)
    table_far = swap_with(table, 1)

    share = cand_ids.shape[1] // size
    my_user = jnp.sum(jnp.where(is_mine, user_range, 0))
    ids = lax.dynamic_slice(cand_ids, (my_user, my_place * share), (1, share))[0]
    owner = ids // pool_here
    differs = (owner % size) ^ my_place
    place = (differs % 2) * rows + (differs // 2) * (rows // 2)
    place = place + ((owner // size) ^ my_group) * pool_here + ids % pool_here
    return call(
        select_kernel,
        shape((share, width), jnp.bfloat16),
        [VMEM] * 3,
        flops=2 * share * 2 * rows * width,
        bytes_accessed=share * width * 2,
        name="select",
    )(place[:, None], table, table_far)


def solution(mesh):
    in_specs = (
        P(("groups", "rank"), None),
        P(("groups", "rank"), None, None, None),
        P(),
        P(),
        P(),
        P("groups", None),
        P(),
        P("groups"),
        P("groups", None),
    )
    out_specs = P(("groups", "rank"), None)
    return jax.shard_map(body, mesh=mesh, in_specs=in_specs, out_specs=out_specs, check_vma=False)
```

```python
import functools
import math

import jax
import jax.numpy as jnp
from jax import lax
from jax.experimental import pallas as pl
from jax.experimental.pallas import tpu as pltpu
from jax.sharding import PartitionSpec as P


norm_eps = 1e-05
VMEM = pl.BlockSpec(memory_space=pltpu.VMEM)
SMEM = pl.BlockSpec(memory_space=pltpu.SMEM)
HBM = pl.BlockSpec(memory_space=pltpu.HBM)


def in_hbm(array):
    return pltpu.with_memory_space_constraint(array, pltpu.HBM)


def swap_with(shard, mask):
    return lax.ppermute(shard, "rank", [(i, i ^ mask) for i in range(lax.axis_size("rank"))])


def call(kernel, out_shape, in_specs, scratch=(), flops=0, bytes_accessed=0):
    single = not isinstance(out_shape, (list, tuple))
    return pl.pallas_call(
        kernel,
        out_shape=out_shape,
        in_specs=in_specs,
        out_specs=VMEM if single else [VMEM] * len(out_shape),
        scratch_shapes=list(scratch),
        compiler_params=pltpu.CompilerParams(vmem_limit_bytes=48 * 1024 * 1024),
        cost_estimate=pl.CostEstimate(flops=flops, bytes_accessed=bytes_accessed, transcendentals=0),
    )


def pick_kernel(groups, size, me_ref, ranker_ref, length_ref, slot_ref, kv_ref, *refs):
    outs, (ranker, length, slots, sem) = refs[:groups], refs[groups:]
    slots_here = kv_ref.shape[0]
    users, blocks = slots.shape
    loads = [
        pltpu.make_async_copy(ref, to, sem.at[i])
        for i, (ref, to) in enumerate(((ranker_ref, ranker), (length_ref, length), (slot_ref, slots)))
    ]
    for load in loads:
        load.start()
    for load in loads:
        load.wait()
    first = me_ref[0] * slots_here
    my_group = me_ref[0] // size

    def held_by(user):
        def step(b, found):
            local = slots[user, b] - first
            here = (local >= 0) & (local < slots_here)
            return jnp.where(here, local, found[0]), jnp.where(here, b, found[1])

        return lax.fori_loop(0, blocks, step, (0, 0), unroll=blocks <= 16)

    def user_of(group):
        def step(u, found):
            return jnp.where(ranker[u] == group, u, found)

        return lax.fori_loop(0, users, step, 0, unroll=users <= 16)

    lives = []
    for k in range(groups):
        user = user_of(my_group ^ k)
        slot, at = held_by(user)
        lives.append(at < length[user])

        @pl.when(lives[k])
        def _(k=k, slot=slot):
            pltpu.make_async_copy(kv_ref.at[slot], outs[k], sem.at[3 + k]).start()

        @pl.when(jnp.logical_not(lives[k]))
        def _(k=k):
            outs[k][...] = jnp.zeros_like(outs[k])

    for k in range(groups):

        @pl.when(lives[k])
        def _(k=k):
            pltpu.make_async_copy(kv_ref.at[0], outs[k], sem.at[3 + k]).wait()


def project(heads, rows_ref, w_ref, q_ref, gate_ref):
    dim = w_ref.shape[1] // (2 * heads)
    qu = jax.nn.silu(jnp.dot(rows_ref[...], w_ref[...], preferred_element_type=jnp.float32))
    qu = qu.astype(jnp.bfloat16)
    for h in range(heads):
        cols = slice(h * dim, (h + 1) * dim)
        q_ref[:, cols] = qu[:, 2 * h * dim : (2 * h + 1) * dim]
        gate_ref[:, cols] = qu[:, (2 * h + 1) * dim : (2 * h + 2) * dim]


def project_kernel(heads, rows_ref, w_ref, q_ref, gate_ref):
    project(heads, rows_ref, w_ref, q_ref, gate_ref)


def project_and_place_kernel(
    heads, size, pool_here, me_ref, rows_ref, w_ref, ranker_ref, ids_ref, q_ref, gate_ref, hot_ref, ranker, ids, sem
):
    users = ids_ref.shape[0]
    share = ids.shape[1]
    me = me_ref[0]
    my_group, my_place = me // size, me % size
    loads = (
        pltpu.make_async_copy(ranker_ref, ranker, sem.at[0]),
        pltpu.make_async_copy(ids_ref.at[:, pl.ds(pl.multiple_of(my_place * share, share), share)], ids, sem.at[1]),
    )
    for load in loads:
        load.start()
    project(heads, rows_ref, w_ref, q_ref, gate_ref)
    for load in loads:
        load.wait()

    def step(u, found):
        return jnp.where(ranker[u] == my_group, u, found)

    my_user = lax.fori_loop(0, users, step, 0, unroll=users <= 16)
    item = ids[pl.ds(my_user, 1), :]
    owner = item // pool_here
    differs = (owner % size) ^ my_place
    rows = hot_ref.shape[1] // 2
    place = (differs % 2) * rows + (differs // 2) * (rows // 2)
    place = place + ((owner // size) ^ my_group) * pool_here + item % pool_here
    part = math.gcd(2 * rows, 256)
    for first in range(0, 2 * rows, part):
        at = lax.broadcasted_iota(jnp.int32, (part, share), 0) + first
        hot = jnp.where(at == place, 1.0, 0.0)
        hot_ref[:, first : first + part] = jnp.transpose(hot).astype(jnp.bfloat16)


def attend_kernel(scale, q_own_ref, q_far_ref, *refs):
    kv, sum_ref, sent_ref = refs[:-2], refs[-2], refs[-1]
    heads, _, pair = kv[0].shape
    dim = pair // 2
    half = q_own_ref.shape[0]
    tile = math.gcd(half, 64)
    together = math.gcd(len(kv), 4)

    def one_tile(t, _):
        at = pl.ds(pl.multiple_of(t * tile, tile), tile)
        low = pl.ds(pl.multiple_of(t * tile + half, tile), tile)
        for h in range(heads):
            cols = slice(h * dim, (h + 1) * dim)
            query = jnp.concatenate([q_own_ref[at, cols], q_far_ref[at, cols]], axis=0)
            total = None
            for first in range(0, len(kv), together):
                parts = [kv[k][h] for k in range(first, first + together)]
                keys = jnp.concatenate([p[:, :dim] for p in parts], axis=0)
                values = jnp.concatenate([p[:, dim:] for p in parts], axis=0)
                scores = lax.dot_general(
                    query, keys, (((1,), (1,)), ((), ())), preferred_element_type=jnp.float32
                )
                weights = jax.nn.silu(scores * scale).astype(jnp.bfloat16)
                add = jnp.dot(weights, values, preferred_element_type=jnp.float32)
                total = add if total is None else total + add
            sum_ref[at, cols] = total[:tile]
            sum_ref[low, cols] = total[tile:]
            sent_ref[at, cols] = total[:tile].astype(jnp.bfloat16)
            sent_ref[low, cols] = total[tile:].astype(jnp.bfloat16)
        return 0

    lax.fori_loop(0, half // tile, one_tile, 0, unroll=half == tile)


def finish_kernel(sum_ref, sent_ref, gate_own_ref, gate_far_ref, own_ref, far_ref, gain_ref, w_ref, out_ref):
    half = own_ref.shape[0]
    tile = math.gcd(half, 64)
    for side, rows, gates in ((0, own_ref, gate_own_ref), (1, far_ref, gate_far_ref)):
        for first in range(0, half, tile):
            mine = slice(side * half + first, side * half + first + tile)
            theirs = slice((1 - side) * half + first, (1 - side) * half + first + tile)
            here = slice(first, first + tile)
            attended = sum_ref[mine, :] + sent_ref[theirs, :].astype(jnp.float32)
            mean = jnp.mean(attended, axis=1, keepdims=True)
            variance = jnp.mean(attended * attended, axis=1, keepdims=True) - mean * mean
            hidden = (attended - mean) * lax.rsqrt(variance + norm_eps) * gain_ref[...]
            hidden = (hidden * gates[here, :].astype(jnp.float32)).astype(jnp.bfloat16)
            mixed = jnp.dot(hidden, w_ref[...], preferred_element_type=jnp.float32)
            mixed = mixed + rows[here, :].astype(jnp.float32)
            out_ref[mine, :] = mixed.astype(jnp.bfloat16)


def select_kernel(hot_ref, own_ref, far_ref, out_ref, buffer, sem):
    rows = own_ref.shape[0]
    share = hot_ref.shape[0]
    tile = math.gcd(share, 128)
    copies = []
    for i, first in enumerate(range(0, share, tile)):
        at = slice(first, first + tile)
        picked = jnp.dot(hot_ref[at, :rows], own_ref[...], preferred_element_type=jnp.float32)
        picked = picked + jnp.dot(hot_ref[at, rows:], far_ref[...], preferred_element_type=jnp.float32)
        buffer[at, :] = picked.astype(jnp.bfloat16)
        copies.append(pltpu.make_async_copy(buffer.at[at], out_ref.at[at], sem.at[i]))
        copies[-1].start()
    for copy in copies:
        copy.wait()


def layer(pool, kv_cache, w_qu, w_out, norm_gain, cand_ids, ranker, hist_blocks, cache_slot):
    devices = lax.axis_size("rank")
    me = lax.axis_index("rank").astype(jnp.int32).reshape(1)
    _, heads, block, pair = kv_cache.shape
    dim = pair // 2
    users, _ = cache_slot.shape
    pool_here, width = pool.shape
    groups = users
    size = devices // groups
    assert size == 4 and groups & (groups - 1) == 0
    shape = jax.ShapeDtypeStruct
    dma = pltpu.SemaphoreType.DMA

    picked = call(
        functools.partial(pick_kernel, groups, size),
        [shape((heads, block, pair), jnp.bfloat16)] * groups,
        [SMEM, HBM, HBM, HBM, HBM],
        [
            pltpu.SMEM(ranker.shape, jnp.int32),
            pltpu.SMEM(hist_blocks.shape, jnp.int32),
            pltpu.SMEM(cache_slot.shape, jnp.int32),
            dma((3 + groups,)),
        ],
        bytes_accessed=2 * kv_cache.size * 2,
    )(me, *[in_hbm(a) for a in (ranker, hist_blocks, cache_slot, kv_cache)])
    column, kv = [pool], [picked[0]]
    for k in range(1, groups):
        column.append(swap_with(pool, size * k))
        kv.append(swap_with(picked[k], size * k))

    own_rows = jnp.concatenate(column, axis=0)
    far_rows = swap_with(own_rows, 2)
    half = own_rows.shape[0]
    rows = 2 * half
    share = cand_ids.shape[1] // size
    cost = dict(flops=2 * half * width * w_qu.shape[1], bytes_accessed=half * width * 4)
    halves = [shape((half, heads * dim), jnp.bfloat16)] * 2
    q_own, gate_own, hot = call(
        functools.partial(project_and_place_kernel, heads, size, pool_here),
        halves + [shape((share, 2 * rows), jnp.bfloat16)],
        [SMEM, VMEM, VMEM, HBM, HBM],
        [pltpu.SMEM(ranker.shape, jnp.int32), pltpu.VMEM((users, share), jnp.int32), dma((2,))],
        **cost,
    )(me, own_rows, w_qu, in_hbm(ranker), in_hbm(cand_ids))
    q_far, gate_far = call(functools.partial(project_kernel, heads), halves, [VMEM] * 2, **cost)(far_rows, w_qu)

    for k in range(groups):
        after = q_own if k < 2 else q_far
        ready, after = lax.optimization_barrier((kv[k], after))
        if k < 2:
            q_own = after
        else:
            q_far = after
        kv.append(swap_with(ready, 1))
    sums, sent = call(
        functools.partial(attend_kernel, 1.0 / math.sqrt(dim)),
        [shape((rows, heads * dim), jnp.float32), shape((rows, heads * dim), jnp.bfloat16)],
        [VMEM] * (2 + len(kv)),
        flops=4 * rows * len(kv) * block * heads * dim,
        bytes_accessed=len(kv) * heads * block * pair * 2,
    )(q_own, q_far, *kv)
    sent = swap_with(sent, 2)
    table = call(
        finish_kernel,
        shape((rows, width), jnp.bfloat16),
        [VMEM] * 8,
        flops=2 * rows * heads * dim * width,
        bytes_accessed=w_out.size * 2,
    )(sums, sent, gate_own, gate_far, own_rows, far_rows, norm_gain[None, :], w_out)
    table_far = swap_with(table, 1)
    return pl.pallas_call(
        select_kernel,
        out_shape=shape((share, width), jnp.bfloat16),
        in_specs=[VMEM] * 3,
        out_specs=HBM,
        scratch_shapes=[pltpu.VMEM((share, width), jnp.bfloat16), dma((share // math.gcd(share, 128),))],
        compiler_params=pltpu.CompilerParams(vmem_limit_bytes=48 * 1024 * 1024),
        cost_estimate=pl.CostEstimate(
            flops=2 * share * 2 * rows * width, bytes_accessed=share * width * 2, transcendentals=0
        ),
        name="select",
    )(hot, table, table_far)


def solution(mesh):
    in_specs = (
        P(("groups", "rank"), None),
        P(("groups", "rank"), None, None, None),
        P(),
        P(),
        P(),
        P("groups", None),
        P(),
        P("groups"),
        P("groups", None),
    )
    out_specs = P(("groups", "rank"), None)
    return jax.shard_map(layer, mesh=mesh, in_specs=in_specs, out_specs=out_specs, check_vma=False)
```

```python
import functools
import math

import jax
import jax.numpy as jnp
from jax import lax
from jax.experimental import pallas as pl
from jax.experimental.pallas import tpu as pltpu
from jax.sharding import PartitionSpec as P


norm_eps = 1e-05
VMEM = pl.BlockSpec(memory_space=pltpu.VMEM)
SMEM = pl.BlockSpec(memory_space=pltpu.SMEM)
HBM = pl.BlockSpec(memory_space=pltpu.HBM)


def in_hbm(array):
    return pltpu.with_memory_space_constraint(array, pltpu.HBM)


def swap_with(shard, mask):
    return lax.ppermute(shard, "rank", [(i, i ^ mask) for i in range(lax.axis_size("rank"))])


def call(kernel, out_shape, in_specs, scratch=(), flops=0, bytes_accessed=0):
    single = not isinstance(out_shape, (list, tuple))
    return pl.pallas_call(
        kernel,
        out_shape=out_shape,
        in_specs=in_specs,
        out_specs=VMEM if single else [VMEM] * len(out_shape),
        scratch_shapes=list(scratch),
        compiler_params=pltpu.CompilerParams(vmem_limit_bytes=24 * 1024 * 1024),
        cost_estimate=pl.CostEstimate(flops=flops, bytes_accessed=bytes_accessed, transcendentals=0),
    )


def pick_kernel(groups, size, me_ref, ranker_ref, length_ref, slot_ref, pool_ref, kv_ref, *refs):
    keep_ref, give_ref, rows_ref, ranker, length, slots, held, sem = refs
    slots_here, heads, _, _ = kv_ref.shape
    count = heads // 2
    core = me_ref[0] % 2
    users, blocks = slots.shape
    pairs = ((ranker_ref, ranker), (length_ref, length), (slot_ref, slots), (pool_ref, rows_ref), (kv_ref, held))
    loads = [pltpu.make_async_copy(ref, to, sem.at[i]) for i, (ref, to) in enumerate(pairs)]
    for load in loads:
        load.start()
    for load in loads[:3]:
        load.wait()
    first = me_ref[0] * slots_here
    my_group = me_ref[0] // size

    def held_by(user):
        def step(b, found):
            local = slots[user, b] - first
            here = (local >= 0) & (local < slots_here)
            return jnp.where(here, local, found[0]), jnp.where(here, b, found[1])

        return lax.fori_loop(0, blocks, step, (0, 0), unroll=blocks <= 16)

    def user_of(group):
        def step(u, found):
            return jnp.where(ranker[u] == group, u, found)

        return lax.fori_loop(0, users, step, 0, unroll=users <= 16)

    chosen = []
    for k in range(groups):
        user = user_of(my_group ^ k)
        slot, at = held_by(user)
        chosen.append((slot, at < length[user]))
    for load in loads[3:]:
        load.wait()
    for k, (slot, live) in enumerate(chosen):
        for i in range(count):
            for out_ref, half in ((keep_ref, core), (give_ref, 1 - core)):
                taken = held[slot, half * count + i]
                out_ref[k, i] = jnp.where(live, taken, jnp.zeros_like(taken))


def pack_kernel(keep_ref, got_ref, *outs):
    for k, out in enumerate(outs):
        out[0] = keep_ref[k]
        out[1] = got_ref[k]


def project(core, heads, rows_ref, w_ref, q_ref, gate_ref, give_ref, halves):
    dim = w_ref.shape[1] // (2 * heads)
    part = heads // 2 * dim
    qu = jax.nn.silu(jnp.dot(rows_ref[...], w_ref[...], preferred_element_type=jnp.float32))
    qu = qu.astype(jnp.bfloat16)
    for h in range(heads):
        at = (2 * h) // heads
        cols = slice(h * dim - at * part, (h + 1) * dim - at * part)
        halves[at, :, cols] = qu[:, 2 * h * dim : (2 * h + 1) * dim]
        gate = qu[:, (2 * h + 1) * dim : (2 * h + 2) * dim]
        gate_ref[:, h * dim : (h + 1) * dim] = gate
        give_ref[:, part + h * dim : part + (h + 1) * dim] = gate
    q_ref[...] = halves[core]
    give_ref[:, :part] = halves[1 - core]
    give_ref[:, 3 * part :] = rows_ref[...]


def project_kernel(heads, me_ref, rows_ref, w_ref, q_ref, gate_ref, give_ref, halves):
    project(me_ref[0] % 2, heads, rows_ref, w_ref, q_ref, gate_ref, give_ref, halves)


def project_and_place_kernel(
    heads, size, me_ref, rows_ref, w_ref, ranker_ref, ids_ref, q_ref, gate_ref, give_ref, hot_ref, halves, ranker, ids, sem
):
    users = ids_ref.shape[0]
    share = ids.shape[1]
    me = me_ref[0]
    my_group, my_place = me // size, me % size
    loads = (
        pltpu.make_async_copy(ranker_ref, ranker, sem.at[0]),
        pltpu.make_async_copy(ids_ref.at[:, pl.ds(pl.multiple_of(my_place * share, share), share)], ids, sem.at[1]),
    )
    for load in loads:
        load.start()
    project(me % 2, heads, rows_ref, w_ref, q_ref, gate_ref, give_ref, halves)
    for load in loads:
        load.wait()

    def step(u, found):
        return jnp.where(ranker[u] == my_group, u, found)

    my_user = lax.fori_loop(0, users, step, 0, unroll=users <= 16)
    item = ids[pl.ds(my_user, 1), :]
    half = rows_ref.shape[0]
    groups = ranker.shape[0]
    pool_here = half // groups
    owner = item // pool_here
    differs = (owner % size) ^ my_place
    place = (differs % 2) * 2 * half + (differs // 2) * half
    apart = (owner // size) ^ my_group
    bit = 1
    while bit < groups:
        place = place + (apart // bit % 2) * (groups // (2 * bit)) * pool_here
        bit *= 2
    place = place + item % pool_here
    part = math.gcd(4 * half, 256)
    for first in range(0, 4 * half, part):
        at = lax.broadcasted_iota(jnp.int32, (part, share), 0) + first
        hot = jnp.where(at == place, 1.0, 0.0)
        hot_ref[:, first : first + part] = jnp.transpose(hot).astype(jnp.bfloat16)


def attend_kernel(scale, q_own_ref, q_far_ref, other_own_ref, other_far_ref, *refs):
    kv, sum_ref, sent_ref = refs[:-2], refs[-2], refs[-1]
    sources, count, _, pair = kv[0].shape
    dim = pair // 2
    half = q_own_ref.shape[0]
    tile = math.gcd(half, 64)
    spots = [(ref, i) for ref in kv for i in range(sources)]
    together = math.gcd(len(spots), 8)

    def one_tile(t, _):
        at = pl.ds(pl.multiple_of(t * tile, tile), tile)
        for h in range(count):
            cols = slice(h * dim, (h + 1) * dim)
            query = jnp.concatenate(
                [ref[at, cols] for ref in (q_own_ref, q_far_ref, other_own_ref, other_far_ref)], axis=0
            )
            total = None
            for first in range(0, len(spots), together):
                parts = [ref[i, h] for ref, i in spots[first : first + together]]
                keys = jnp.concatenate([p[:, :dim] for p in parts], axis=0)
                values = jnp.concatenate([p[:, dim:] for p in parts], axis=0)
                scores = lax.dot_general(
                    query, keys, (((1,), (1,)), ((), ())), preferred_element_type=jnp.float32
                )
                weights = jax.nn.silu(scores * scale).astype(jnp.bfloat16)
                add = jnp.dot(weights, values, preferred_element_type=jnp.float32)
                total = add if total is None else total + add
            for i in range(4):
                here = pl.ds(pl.multiple_of(t * tile + i * half, tile), tile)
                piece = total[i * tile : (i + 1) * tile]
                sum_ref[here, cols] = piece
                sent_ref[here, cols] = piece.astype(jnp.bfloat16)
        return 0

    lax.fori_loop(0, half // tile, one_tile, 0, unroll=half == tile)


def combine_kernel(sum_ref, got_ref, out_ref):
    half = sum_ref.shape[0] // 4
    for i in range(4):
        here, there = slice(i * half, (i + 1) * half), slice((i ^ 1) * half, ((i ^ 1) + 1) * half)
        out_ref[here, :] = sum_ref[here, :] + got_ref[there, :].astype(jnp.float32)


def finish_kernel(
    me_ref, att_ref, far_ref, gate_own_ref, gate_far_ref, own_ref, far_rows_ref, other_own_ref, other_far_ref,
    gain_ref, w_ref, hot_ref, out_ref, table, buffer, sem
):
    core = me_ref[0] % 2
    half, width = own_ref.shape
    part = att_ref.shape[1]
    tile = math.gcd(half, 64)
    w_mine = w_ref[pl.ds(pl.multiple_of(core * part, part), part), :]
    w_other = w_ref[pl.ds(pl.multiple_of((1 - core) * part, part), part), :]
    low, high = gain_ref[:, :part], gain_ref[:, part:]
    gain_mine, gain_other = jnp.where(core == 0, low, high), jnp.where(core == 0, high, low)
    pieces = (
        (gate_own_ref, 0, own_ref, 0),
        (gate_far_ref, 0, far_rows_ref, 0),
        (other_own_ref, part, other_own_ref, 3 * part),
        (other_far_ref, part, other_far_ref, 3 * part),
    )
    for i, (gates, gate_at, rows, rows_at) in enumerate(pieces):
        for first in range(0, half, tile):
            mine = slice(i * half + first, i * half + first + tile)
            theirs = slice((i ^ 2) * half + first, (i ^ 2) * half + first + tile)
            here = slice(first, first + tile)
            a, b = att_ref[mine, :], far_ref[theirs, :]
            mean = (jnp.sum(a, axis=1, keepdims=True) + jnp.sum(b, axis=1, keepdims=True)) * (0.5 / part)
            square = (jnp.sum(a * a, axis=1, keepdims=True) + jnp.sum(b * b, axis=1, keepdims=True)) * (0.5 / part)
            factor = lax.rsqrt(square - mean * mean + norm_eps)
            low = gates[here, gate_at : gate_at + part].astype(jnp.float32)
            high = gates[here, gate_at + part : gate_at + 2 * part].astype(jnp.float32)
            g_mine, g_other = jnp.where(core == 0, low, high), jnp.where(core == 0, high, low)
            a = ((a - mean) * factor * gain_mine * g_mine).astype(jnp.bfloat16)
            b = ((b - mean) * factor * gain_other * g_other).astype(jnp.bfloat16)
            mixed = jnp.dot(a, w_mine, preferred_element_type=jnp.float32)
            mixed = mixed + jnp.dot(b, w_other, preferred_element_type=jnp.float32)
            mixed = mixed + rows[here, rows_at : rows_at + width].astype(jnp.float32)
            table[mine, :] = mixed.astype(jnp.bfloat16)
    share = hot_ref.shape[0]
    tile = math.gcd(share, 128)
    copies = []
    for i, first in enumerate(range(0, share, tile)):
        at = slice(first, first + tile)
        buffer[at, :] = jnp.dot(hot_ref[at, :], table[...], preferred_element_type=jnp.float32).astype(jnp.bfloat16)
        copies.append(pltpu.make_async_copy(buffer.at[at], out_ref.at[at], sem.at[i]))
        copies[-1].start()
    for copy in copies:
        copy.wait()


def layer(pool, kv_cache, w_qu, w_out, norm_gain, cand_ids, ranker, hist_blocks, cache_slot):
    devices = lax.axis_size("rank")
    me = lax.axis_index("rank").astype(jnp.int32).reshape(1)
    _, heads, block, pair = kv_cache.shape
    dim = pair // 2
    users, _ = cache_slot.shape
    _, width = pool.shape
    groups = users
    size = devices // groups
    assert size == 4 and groups & (groups - 1) == 0
    shape = jax.ShapeDtypeStruct
    dma = pltpu.SemaphoreType.DMA

    count = heads // 2
    blocks_shape = shape((groups, count, block, pair), jnp.bfloat16)
    keep, give, pool_rows = call(
        functools.partial(pick_kernel, groups, size),
        [blocks_shape, blocks_shape, shape(pool.shape, pool.dtype)],
        [SMEM] + [HBM] * 5,
        [
            pltpu.SMEM(ranker.shape, jnp.int32),
            pltpu.SMEM(hist_blocks.shape, jnp.int32),
            pltpu.SMEM(cache_slot.shape, jnp.int32),
            pltpu.VMEM(kv_cache.shape, kv_cache.dtype),
            dma((5,)),
        ],
        bytes_accessed=2 * kv_cache.size * 2,
    )(me, *[in_hbm(a) for a in (ranker, hist_blocks, cache_slot, pool, kv_cache)])
    got = swap_with(give, 1)
    own_rows, sent = pool_rows, pool
    bit = groups // 2
    while bit:
        if bit < groups // 2:
            sent, got = lax.optimization_barrier((own_rows, got))
        own_rows = jnp.concatenate([own_rows, swap_with(sent, size * bit)], axis=0)
        bit //= 2
    kv = call(pack_kernel, [shape((2, count, block, pair), jnp.bfloat16)] * groups, [VMEM] * 2)(keep, got)
    kv = list(kv)
    for k in range(1, groups):
        kv[k] = swap_with(kv[k], size * k)

    far_rows = swap_with(own_rows, 2)
    half = own_rows.shape[0]
    rows = 4 * half
    part = count * dim
    share = cand_ids.shape[1] // size
    cost = dict(flops=2 * half * width * w_qu.shape[1], bytes_accessed=half * width * 4)
    outs = [shape((half, n), jnp.bfloat16) for n in (part, 2 * part, 3 * part + width)]
    halves = pltpu.VMEM((2, half, part), jnp.bfloat16)
    q_own, gate_own, give_own, hot = call(
        functools.partial(project_and_place_kernel, heads, size),
        outs + [shape((share, rows), jnp.bfloat16)],
        [SMEM, VMEM, VMEM, HBM, HBM],
        [halves, pltpu.SMEM(ranker.shape, jnp.int32), pltpu.VMEM((users, share), jnp.int32), dma((2,))],
        **cost,
    )(me, own_rows, w_qu, in_hbm(ranker), in_hbm(cand_ids))
    other_own = swap_with(give_own, 1)
    q_far, gate_far, give_far = call(
        functools.partial(project_kernel, heads), outs, [SMEM, VMEM, VMEM], [halves], **cost
    )(me, far_rows, w_qu)
    other_far = swap_with(give_far, 1)

    sums, sent = call(
        functools.partial(attend_kernel, 1.0 / math.sqrt(dim)),
        [shape((rows, part), jnp.float32), shape((rows, part), jnp.bfloat16)],
        [VMEM] * (4 + groups),
        flops=4 * rows * 2 * groups * block * part,
        bytes_accessed=2 * groups * count * block * pair * 2,
    )(q_own, q_far, other_own, other_far, *kv)
    sent = swap_with(sent, 2)
    attended = call(combine_kernel, shape((rows, part), jnp.float32), [VMEM] * 2)(sums, sent)
    other = swap_with(attended, 1)
    return pl.pallas_call(
        finish_kernel,
        out_shape=shape((share, width), jnp.bfloat16),
        in_specs=[SMEM] + [VMEM] * 11,
        out_specs=HBM,
        scratch_shapes=[
            pltpu.VMEM((rows, width), jnp.bfloat16),
            pltpu.VMEM((share, width), jnp.bfloat16),
            dma((share // math.gcd(share, 128),)),
        ],
        compiler_params=pltpu.CompilerParams(vmem_limit_bytes=24 * 1024 * 1024),
        cost_estimate=pl.CostEstimate(
            flops=2 * (share * rows + rows * heads * dim) * width, bytes_accessed=share * width * 2, transcendentals=0
        ),
        name="finish",
    )(
        me, attended, other, gate_own, gate_far, own_rows, far_rows, other_own, other_far,
        norm_gain[None, :], w_out, hot,
    )


def solution(mesh):
    in_specs = (
        P(("groups", "rank"), None),
        P(("groups", "rank"), None, None, None),
        P(),
        P(),
        P(),
        P("groups", None),
        P(),
        P("groups"),
        P("groups", None),
    )
    out_specs = P(("groups", "rank"), None)
    return jax.shard_map(layer, mesh=mesh, in_specs=in_specs, out_specs=out_specs, check_vma=False)
```
